32 devices in a mesh: dp: 8 (over z, y), sub: 4 (over x, core).
Axes of the slice: x: 2, y: 2, z: 4, core: 2. Of those that a mesh axis runs over, the one named last changes fastest.
Arguments:
- vectors: bfloat16 [4096, 2048], P(('dp', 'sub')), may hold values from -6 to 6
- rotation: bfloat16 [2048, 2048], P(None, 'sub'), may hold values from -0.125 to 0.125
- codebook: bfloat16 [16, 4096, 128], P('sub'), may hold values from -6 to 6
- codes: int32 [4096, 16], P('dp', 'sub'), may hold values from 0 to 4095
Outputs:
- centroids: bfloat16 [16, 4096, 128], P('sub')
- distortion: float32 [4096, 16], P('dp', 'sub')
- cross: float32 [2048, 2048], P('dp', 'sub')
The draws below stay inside these ranges and needn't reach their ends.
All inputs are finite; a program needn't handle non-finite values.
Results may differ from the reference program's by a relative error of at most 0.0047.
Values may be sent and summed in bfloat16 or wider, within the bound.
No kernel may reach another device: no remote copies, remote signals or barrier semaphores. Data moves between devices by JAX's collectives and lax.ppermute only.
A program may use at most 64 MiB of HBM per device.

```python
import jax
import jax.numpy as jnp
from jax import lax

D = 2048
M = 16
K = 4096
DS = 128
ROWS = 4096


def set_ends(array, own_key, smallest, largest):
    extent = array.shape
    place = [jax.random.randint(jax.random.fold_in(own_key, axis), (), 0, extent[axis]) for axis in range(len(extent))]
    array = array.at[tuple(place)].set(smallest)
    longest = extent.index(max(extent))
    place[longest] = (place[longest] + 1) % extent[longest]
    return array.at[tuple(place)].set(largest)


def spiked(result, key, source, target, shards_of, factor):
    def block_of(dim):
        return (jnp.arange(result.shape[dim]) // (result.shape[dim] // shards_of)).reshape((-1,) + (1,) * (result.ndim - 1 - dim))

    near = jax.random.permutation(key, shards_of)[block_of(target)]
    far = (block_of(target) + shards_of // 2) % shards_of
    return jnp.where((block_of(source) == near) | (block_of(source) == far), factor * result, result)


def block_levels(key, dims, split, low, top_value):
    factor_of, own = 1.0, jax.random.fold_in(key, 6)
    for axis_at, shards_of in split:
        draws = jnp.exp(jax.random.uniform(jax.random.fold_in(own, axis_at), (shards_of,), jnp.float32, low / len(split), top_value / len(split)))
        factor_of = factor_of * jnp.repeat(draws, dims[axis_at] // shards_of).reshape([-1 if axis == axis_at else 1 for axis in range(len(dims))])
    return factor_of


def gaussian(rng, extent, deviation, reach, cuts=(), kind=jnp.bfloat16):
    drawn = jax.random.normal(rng, extent, jnp.float32) * deviation
    if len(cuts) > 0:
        drawn = block_levels(rng, extent, cuts, -0.22, 0.18) * drawn
    return jnp.clip(drawn, min=-reach, max=reach).astype(kind)


def heavy_noise(key, dims, deviation, bound, cuts, heavy, kind=jnp.bfloat16):
    array = deviation * jax.random.normal(key, dims, jnp.float32)
    if cuts:
        array = array * block_levels(key, dims, cuts, -0.22, 0.18)
    return jnp.clip(spiked(array, jax.random.fold_in(key, 3), *heavy), -bound, bound).astype(kind)


def setup_inputs(seed: int = 0) -> dict:
    seeds = jax.random.split(jax.random.key(seed), 5)
    return {
        "vectors": heavy_noise(seeds[0], (ROWS, D), 1.0, 6.0, ((0, 32),), (0, 1, 32, 2.75)),
        "rotation": gaussian(seeds[1], (D, D), D ** -0.5, 0.125, ((1, 4),)),
        "codebook": gaussian(seeds[2], (M, K, DS), 1.0, 6.0, ((0, 4),)),
        "codes": set_ends(jax.random.randint(seeds[3], (ROWS, M), 0, K), jax.random.fold_in(seeds[3], 1), 0, K - 1).astype(jnp.int32),
    }


def one_subspace(operands):
    values, labels, codewords = operands
    count = codewords.shape[0]
    totals = jax.ops.segment_sum(values.astype(jnp.float32), labels, num_segments=count)
    members = jax.ops.segment_sum(jnp.ones(labels.shape, jnp.float32), labels, num_segments=count)
    centroid = ((totals + codewords.astype(jnp.float32)) / (members[:, None] + 1.0)).astype(jnp.bfloat16)
    rebuilt = jnp.take(centroid, labels, axis=0)
    distance = jnp.sum((values.astype(jnp.float32) - rebuilt.astype(jnp.float32)) ** 2, axis=-1)
    return centroid, rebuilt, distance


def reference(vectors, rotation, codebook, codes):
    total_rows = vectors.shape[0]
    rotated = jnp.dot(vectors, rotation, preferred_element_type=jnp.float32).astype(jnp.bfloat16)
    pieces = rotated.reshape(total_rows, M, DS).transpose(1, 0, 2)
    centroid, rebuilt, distance = lax.map(one_subspace, (pieces, codes.T.astype(jnp.int32), codebook))
    rebuilt_rows = rebuilt.transpose(1, 0, 2).reshape(total_rows, D)
    cross = lax.dot_general(vectors, rebuilt_rows, (((0,), (0,)), ((), ())), preferred_element_type=jnp.float32)
    return centroid, distance.T, cross
```

```python
import functools

import jax
import jax.numpy as jnp
from jax import lax
from jax.experimental import pallas as pl
from jax.experimental.pallas import tpu as pltpu
from jax.sharding import PartitionSpec as P

F32 = jnp.float32
BF16 = jnp.bfloat16
ANY = pl.BlockSpec(memory_space=pl.ANY)
VMEM = pl.BlockSpec(memory_space=pltpu.VMEM)
SMEM = pl.BlockSpec(memory_space=pltpu.SMEM)


def rotate_kernel(own_ref, *refs):
    *piece_refs, rotation_ref, out_ref = refs
    rows = piece_refs[0].shape[0]
    groups, _, width = out_ref.shape
    for piece, ref in enumerate(piece_refs):
        product = jnp.dot(ref[...], rotation_ref[...], preferred_element_type=F32)
        for q in range(groups):
            out_ref[q ^ own_ref[0], piece * rows : (piece + 1) * rows, :] = product[
                :, q * width : (q + 1) * width
            ].astype(BF16)


def rotate(own, pieces, rotation, groups):
    rows = pieces[0].shape[0]
    width = rotation.shape[1] // groups
    return pl.pallas_call(
        rotate_kernel,
        out_shape=jax.ShapeDtypeStruct((groups, len(pieces) * rows, width), BF16),
        in_specs=[SMEM] + [VMEM] * (len(pieces) + 1),
        out_specs=VMEM,
        cost_estimate=pl.CostEstimate(
            flops=2 * len(pieces) * rows * rotation.size,
            bytes_accessed=2 * (len(pieces) * pieces[0].size + rotation.size),
            transcendentals=0,
        ),
        name="rotate",
    )(own, *pieces, rotation)


def update_kernel(place_ref, codes_ref, values_ref, codebook_ref, out_ref, total_ref):
    tile, width = out_ref.shape
    chunk = values_ref.shape[0]
    step, last = pl.program_id(1), pl.num_programs(1) - 1

    @pl.when(step == 0)
    def _():
        total_ref[...] = jnp.zeros_like(total_ref)

    first = place_ref[1] + pl.program_id(0) * tile
    slot = lax.broadcasted_iota(jnp.int32, (tile, chunk), 0)
    hit = jnp.where(slot == codes_ref[...] - first, 1.0, 0.0).astype(BF16)
    ones = jnp.ones((chunk, width), BF16)
    total_ref[...] += jnp.dot(
        hit, jnp.concatenate([values_ref[...], ones], axis=1), preferred_element_type=F32
    )

    @pl.when(step == last)
    def _():
        out_ref[...] = (
            (total_ref[:, :width] + codebook_ref[0].astype(F32)) / (total_ref[:, width:] + 1.0)
        ).astype(BF16)


def update(place, codes, values, codebook, owned):
    rows, width = values.shape
    chunk, tile = min(rows, 4096), min(owned, 256)
    per = owned // tile
    return pl.pallas_call(
        update_kernel,
        out_shape=jax.ShapeDtypeStruct((owned, width), BF16),
        grid_spec=pltpu.PrefetchScalarGridSpec(
            num_scalar_prefetch=1,
            grid=(per, rows // chunk),
            in_specs=[
                pl.BlockSpec((1, chunk), lambda k, r, place: (0, r)),
                pl.BlockSpec((chunk, width), lambda k, r, place: (r, 0)),
                pl.BlockSpec((1, tile, width), lambda k, r, place: (place[0], place[2] * per + k, 0)),
            ],
            out_specs=pl.BlockSpec((tile, width), lambda k, r, place: (k, 0)),
            scratch_shapes=[pltpu.VMEM((tile, 2 * width), F32)],
        ),
        cost_estimate=pl.CostEstimate(
            flops=4 * owned * rows * width, bytes_accessed=2 * rows * width, transcendentals=0
        ),
        name="update",
    )(place, codes, values, codebook)


def stage_kernel(split, place_ref, codes_ref, values_ref, *refs):
    pieces, blocks, (outs, scratch) = refs[: split[0]], refs[split[0] : split[0] + split[1]], (
        refs[split[0] + split[1] + split[2] :][:3],
        refs[split[0] + split[1] + split[2] + 3 :],
    )
    centroid_ref, cross_ref, distance_ref = outs
    table, picked, product, block_sems, cross_sem = scratch
    group, half, own = place_ref[0], place_ref[1], place_ref[2]
    owned, width = blocks[0].shape
    parts, rows = pieces[0].shape[0], pieces[0].shape[2]
    chunk = len(pieces) * rows
    copies = []
    for j, block in enumerate(blocks):
        first = lax.rem(half + j, len(blocks)) * owned
        copies.append(
            pltpu.make_async_copy(
                block,
                centroid_ref.at[group, pl.ds(pl.multiple_of(first, owned), owned), :],
                block_sems.at[j],
            )
        )
        copies[-1].start()
        table[j * owned : (j + 1) * owned, :] = block[...].astype(F32)
    product[...] = jnp.zeros_like(product)
    unroll = 32

    def part(p, _):
        def pick(i, _):
            base = pl.multiple_of(i * unroll, unroll)
            for u in range(unroll):
                code = codes_ref[p * chunk + base + u]
                picked[pl.ds(base + u, 1), :] = table[pl.ds(code, 1), :]
            return 0

        lax.fori_loop(0, chunk // unroll, pick, 0)
        left = jnp.concatenate([piece[p] for piece in pieces], axis=1)
        product[...] += jnp.dot(left, picked[...].astype(BF16), preferred_element_type=F32)

        @pl.when(p == own)
        def _():
            gap = values_ref[0].astype(F32) - picked[...]
            distance_ref[...] = jnp.sum(gap * gap, axis=1, keepdims=True)

        return 0

    lax.fori_loop(0, parts, part, 0)
    out = pltpu.make_async_copy(
        product, cross_ref.at[:, pl.ds(pl.multiple_of(group * width, width), width)], cross_sem
    )
    out.start()
    out.wait()
    for copy in copies:
        copy.wait()


def stage(place, codes, values, pieces, blocks, carried, shapes):
    groups, count, width = shapes
    owned = blocks[0].shape[0]
    depth, rows = pieces[0].shape[1:]
    chunk = len(pieces) * rows
    fixed = 3 + len(pieces) + len(blocks)
    return pl.pallas_call(
        functools.partial(stage_kernel, (len(pieces), len(blocks), len(carried))),
        out_shape=(
            jax.ShapeDtypeStruct((groups, count, width), BF16),
            jax.ShapeDtypeStruct((depth, groups * width), F32),
            jax.ShapeDtypeStruct((chunk, 1), F32),
        ),
        in_specs=[SMEM, SMEM, pl.BlockSpec((1, chunk, width), lambda: (0, 0, 0))]
        + [VMEM] * (len(pieces) + len(blocks))
        + [ANY] * len(carried),
        out_specs=(ANY, ANY, VMEM),
        scratch_shapes=[
            pltpu.VMEM((count, width), F32),
            pltpu.VMEM((chunk, width), F32),
            pltpu.VMEM((depth, width), F32),
            pltpu.SemaphoreType.DMA((len(blocks),)),
            pltpu.SemaphoreType.DMA,
        ],
        input_output_aliases={fixed + j: j for j in range(len(carried))},
        cost_estimate=pl.CostEstimate(
            flops=2 * depth * width * codes.size * 32,
            bytes_accessed=4 * codes.size * width,
            transcendentals=0,
        ),
        name="stage",
    )(place, codes, values, *pieces, *blocks, *carried)


def hop(value, axis, pairs, name):
    with jax.named_scope(name):
        return lax.ppermute(value, axis, pairs)


def spread(own, size, axis, name):
    have = {0: own}
    bit = size // 2
    while bit:
        pairs = [(i, i ^ bit) for i in range(size)]
        for offset in sorted(have):
            have[offset ^ bit] = hop(have[offset], axis, pairs, f"{name}{offset ^ bit}")
        bit //= 2
    return [have[o] for o in range(size)]


def per_device(n_dp, n_sub, vectors, rotation, codebook, codes):
    groups, count, width = codebook.shape
    rows, depth = vectors.shape
    halves = n_dp // groups
    owned = count // halves
    paired = halves == 2
    ring = list(range(0, n_dp, 2)) + list(range(n_dp - 1, 0, -2)) if paired else list(range(n_dp))
    at = [ring.index(d) for d in range(n_dp)]
    d, sub = lax.axis_index("dp"), lax.axis_index("sub")
    position = jnp.array(at, jnp.int32)[d]
    group, half = position // halves, position % halves

    pieces = spread(vectors, n_sub, "sub", "rows")
    order = jnp.arange(n_sub, dtype=jnp.int32) ^ sub
    mine = codes.reshape(n_sub, rows, groups)[order].reshape(n_sub * rows, groups).T
    labels = lax.all_to_all(
        jnp.broadcast_to(mine[None], (n_dp,) + mine.shape), "dp", 0, 0, tiled=True
    )
    flipped = vectors.T.reshape(n_dp, depth // n_dp, rows)
    turned = lax.all_to_all(flipped, "dp", 0, 0, tiled=True)

    values = rotate(group.reshape(1), pieces, rotation, groups)
    sides = spread(turned, n_sub, "sub", "side")

    parts = [values[0]]
    for t in range(1, groups):
        pairs = [(ring[p], ring[((p // halves) ^ t) * halves + p % halves]) for p in range(n_dp)]
        parts.append(hop(values[t], "dp", pairs, f"swap{t}"))
    whole = [jnp.concatenate(parts, axis=0)]
    bit = 1
    while bit < halves:
        pairs = [(ring[p], ring[(p // halves) * halves + ((p % halves) ^ bit)]) for p in range(n_dp)]
        whole = whole + [hop(w, "dp", pairs, f"join{bit}") for w in whole]
        bit *= 2
    gathered = jnp.concatenate(whole, axis=0)
    source = jnp.array(
        [
            [
                ring[((p // halves) ^ t) * halves + ((p % halves) ^ e)]
                for e in range(halves)
                for t in range(groups)
            ]
            for p in range(n_dp)
        ],
        jnp.int32,
    )[position]
    by_group = labels.transpose(1, 0, 2)
    own_labels = lax.dynamic_index_in_dim(by_group, group, 0, keepdims=False)[source]
    place = jnp.stack([group, half * owned, half]).astype(jnp.int32)
    block = update(place, own_labels.reshape(1, -1), gathered, codebook, owned)

    shapes = codebook.shape
    carried, distances, seen = (), [], []

    def finish(target, turn, blocks, carried):
        label = lax.dynamic_index_in_dim(by_group, target, 0, keepdims=False).reshape(-1)
        label = (label + (count - turn * owned)) % count
        value = lax.dynamic_index_in_dim(values, target ^ group, 0)
        spot = jnp.stack([target, turn, d]).astype(jnp.int32)
        return stage(spot, label, value, sides, blocks, carried, shapes)

    if paired:
        inner = [(ring[p], ring[p ^ 1]) for p in range(n_dp)]
        outer = [(ring[p], ring[(p - 1 if p % 2 == 0 else p + 1) % n_dp]) for p in range(n_dp)]
        a, b = block, block
        for s in range(1, groups + 1):
            if s < groups:
                a_next = hop(b, "dp", inner, f"inner{s}")
                b_next = hop(a, "dp", outer, f"outer{s}")
            else:
                cut = owned // 2
                a_next = jnp.concatenate(
                    [hop(b[:cut], "dp", inner, f"inner{s}"), hop(a[cut:], "dp", outer, f"outer{s}")],
                    axis=0,
                )
                b_next = a_next
            sign = 1 - 2 * half
            if s % 2:
                target, blocks = (group + sign * ((s - 1) // 2)) % groups, [a, a_next]
            else:
                target, blocks = (group - sign * (s // 2)) % groups, [b_next, b]
            a, b = a_next, b_next
            *carried, distance = finish(target, half, blocks, carried)
            distances.append(distance)
            seen.append(target)
    else:
        table = lax.all_gather(block, "dp", axis=0, tiled=True).reshape(groups, count, width)
        for g in range(groups):
            target = jnp.int32(g)
            *carried, distance = finish(target, jnp.int32(0), [table[g]], carried)
            distances.append(distance)
            seen.append(target)
    centroid, cross = carried
    distance = jnp.stack([x.reshape(n_sub, rows) for x in distances])
    slot = jnp.argmax(jnp.stack(seen)[None] == jnp.arange(groups)[:, None], axis=1)
    distance = distance[slot][:, order].reshape(groups, n_sub * rows)
    return centroid, distance.T, cross


def solution(mesh):
    placed = (P(("dp", "sub"), None), P(None, "sub"), P("sub", None, None), P("dp", "sub"))
    return jax.shard_map(
        functools.partial(per_device, mesh.shape["dp"], mesh.shape["sub"]),
        mesh=mesh,
        in_specs=placed,
        out_specs=(P("sub", None, None), P("dp", "sub"), P("dp", "sub")),
        check_vma=False,
    )
```

```python
import functools

import jax
import jax.numpy as jnp
from jax import lax
from jax.experimental import pallas as pl
from jax.experimental.pallas import tpu as pltpu
from jax.sharding import PartitionSpec as P


F32 = jnp.float32
BF16 = jnp.bfloat16
ANY = pl.BlockSpec(memory_space=pl.ANY)
HBM = pl.BlockSpec(memory_space=pltpu.HBM)
VMEM = pl.BlockSpec(memory_space=pltpu.VMEM)
LANE = 128


def limit(mebibytes):
    return pltpu.CompilerParams(vmem_limit_bytes=mebibytes << 20)


class Plan:
    def __init__(self, n_dp, n_sub, codebook, vectors):
        self.n_dp, self.n_sub = n_dp, n_sub
        self.groups, self.count, self.width = codebook.shape
        self.rows, self.depth = vectors.shape
        self.halves = n_dp // self.groups
        self.owned = self.count // self.halves
        self.paired = self.halves == 2
        self.ring = [self.member(p) for p in range(n_dp)]
        self.chunk = n_sub * self.rows
        self.side = self.chunk // 2
        self.extra = -(-2 * self.side // LANE // 16) * 16
        self.band = self.depth // n_dp

    def member(self, p):
        if not self.paired:
            return p
        if isinstance(p, int):
            return 2 * p if 2 * p < self.n_dp else 2 * (self.n_dp - 1 - p) + 1
        return jnp.where(2 * p < self.n_dp, 2 * p, 2 * (self.n_dp - 1 - p) + 1)

    def mirror(self, group):
        return (2 * group) // self.groups if self.paired else 0 * group

    def here(self):
        d = lax.axis_index("dp")
        if self.paired:
            p = jnp.where(lax.rem(d, 2) == 0, lax.div(d, 2), self.n_dp - 1 - lax.div(d, 2))
        else:
            p = d
        return d, lax.div(p, self.halves), lax.rem(p, self.halves)

    def target(self, step, group, half):
        if not self.paired:
            return step - 1
        away = (step - 1) // 2 if step % 2 else -(step // 2)
        return lax.rem(group + (1 - 2 * half) * away + self.groups, self.groups)


def digits(codes):
    codes = codes.astype(F32)
    high = jnp.floor(codes * (1.0 / LANE))
    return high, codes - high * LANE


def flip_kernel(plan, vectors_ref, codes_ref, out_ref, vectors, codes, sems):
    loads = [
        pltpu.make_async_copy(source, target, sems.at[j])
        for j, (source, target) in enumerate([(vectors_ref, vectors), (codes_ref, codes)])
    ]
    for load in loads:
        load.start()
    band = plan.band
    loads[0].wait()
    for p in range(plan.n_dp):
        out_ref[p, :band, :] = jnp.transpose(vectors[:, p * band : (p + 1) * band])
    loads[1].wait()
    rows = jnp.concatenate([codes[:, j : j + LANE] for j in range(0, plan.chunk, LANE)], axis=0)
    both = jnp.concatenate(digits(rows), axis=0).astype(BF16)
    for p in range(plan.n_dp):
        out_ref[p, band:, :] = both


def flip(plan, vectors, codes):
    extra = 2 * codes.size // LANE
    return pl.pallas_call(
        functools.partial(flip_kernel, plan),
        out_shape=jax.ShapeDtypeStruct((plan.n_dp, plan.band + extra, plan.rows), BF16),
        in_specs=[HBM, HBM],
        out_specs=VMEM,
        scratch_shapes=[
            pltpu.VMEM(vectors.shape, BF16),
            pltpu.VMEM(codes.shape, jnp.int32),
            pltpu.SemaphoreType.DMA((2,)),
        ],
        compiler_params=limit(60),
        name="flip",
    )(vectors, codes)


def pack_kernel(*refs):
    *part_refs, out_ref = refs
    rows = part_refs[0].shape[0]
    for j, part_ref in enumerate(part_refs):
        out_ref[j * rows : (j + 1) * rows, :] = part_ref[...]


def pack(parts):
    rows, width = parts[0].shape
    return pl.pallas_call(
        pack_kernel,
        out_shape=jax.ShapeDtypeStruct((len(parts) * rows, width), BF16),
        in_specs=[VMEM] * len(parts),
        out_specs=VMEM,
        compiler_params=limit(6),
        name="pack",
    )(*parts)


def rotate_kernel(plan, part, offsets, *refs):
    piece_refs = refs[: len(offsets)]
    rotation_ref, codes_ref, out_ref, *part_refs, held = refs[len(offsets) :]
    _, group, _ = plan.here()
    sub = lax.axis_index("sub")
    width, side, extra = plan.width, plan.side, plan.extra
    first = lax.div(sub, plan.n_sub // 2) ^ part
    high, low = digits(codes_ref[:, pl.ds(pl.multiple_of(first * side, side), side)])
    for q in range(plan.groups):
        rows = [x[q : q + 1, j : j + LANE] for x in (high, low) for j in range(0, side, LANE)]
        if len(rows) < extra:
            rows.append(jnp.zeros((extra - len(rows), LANE), F32))
        held[q ^ group, side:, :] = jnp.concatenate(rows, axis=0).astype(BF16)
    for offset, piece_ref in zip(offsets, piece_refs):
        row = pl.multiple_of(lax.rem(sub ^ offset, plan.n_sub // 2) * plan.rows, plan.rows)
        product = jnp.dot(piece_ref[...], rotation_ref[...], preferred_element_type=F32)
        for q in range(plan.groups):
            part = product[:, q * width : (q + 1) * width].astype(BF16)
            out_ref[q, pl.ds(row, plan.rows), :] = part
            held[q ^ group, pl.ds(row, plan.rows), :] = part
    for t, part_ref in enumerate(part_refs):
        part_ref[...] = held[t]


def rotate(plan, part, offsets, pieces, rotation, codes, room):
    shape = (plan.side + plan.extra, plan.width)
    every = jax.ShapeDtypeStruct((plan.groups, plan.side, plan.width), BF16)
    return pl.pallas_call(
        functools.partial(rotate_kernel, plan, part, offsets),
        out_shape=[every] + [jax.ShapeDtypeStruct(shape, BF16)] * plan.groups,
        in_specs=[VMEM] * (len(pieces) + 2),
        out_specs=[VMEM] * (1 + plan.groups),
        scratch_shapes=[pltpu.VMEM((plan.groups, *shape), BF16)],
        compiler_params=limit(room),
        cost_estimate=pl.CostEstimate(
            flops=2 * len(pieces) * plan.rows * rotation.size,
            bytes_accessed=2 * (len(pieces) * pieces[0].size + rotation.size),
            transcendentals=0,
        ),
        name="rotate",
    )(*pieces, rotation, codes)


def update_kernel(plan, count, more, last, *refs):
    value_refs, refs = refs[:count], refs[count:]
    total_ref, refs = (refs[0], refs[1:]) if more else (None, refs)
    codebook_ref, refs = (refs[0], refs[1:]) if last else (None, refs)
    out_refs, (codes, *scratch) = refs[: 1 + last], refs[1 + last :]
    _, group, half = plan.here()
    width, owned, side, extra = plan.width, plan.owned, plan.side, plan.extra
    if last:
        words, sem = scratch
        copy = pltpu.make_async_copy(
            codebook_ref.at[group, pl.ds(pl.multiple_of(half * owned, owned), owned), :], words, sem
        )
        copy.start()
    starts = [(ref, t * (side + extra)) for ref in value_refs for t in range(plan.groups)]
    place, rows = 0, side // LANE
    for ref, start in starts:
        both = ref[start + side : start + side + extra, :].astype(F32)
        codes_here = (both[:rows] * LANE + both[rows : 2 * rows]).astype(jnp.int32)
        for j in range(rows):
            codes[:, place : place + LANE] = codes_here[j : j + 1]
            place += LANE
    part = owned // len(out_refs)
    tile = min(part, 512)
    if last:
        copy.wait()

    def one(out_ref, base, k, _):
        here = pl.multiple_of(k * tile, tile)
        first = pl.multiple_of(base + here, tile)
        slot = lax.broadcasted_iota(jnp.int32, (tile, 1), 0) + (half * owned + first)
        total = total_ref[pl.ds(first, tile), :] if more else jnp.zeros((tile, 2 * width), F32)
        batch = max(1024 // side, 1)
        for j in range(0, len(starts), batch):
            some = starts[j : j + batch]
            place, size = j * side, len(some) * side
            hit = jnp.where(slot == codes[:, place : place + size], 1.0, 0.0).astype(BF16)
            right = jnp.concatenate([ref[start : start + side, :] for ref, start in some], axis=0)
            right = jnp.concatenate([right, jnp.ones((size, width), BF16)], axis=1)
            total += jnp.dot(hit, right, preferred_element_type=F32)
        if last:
            total = (
                (total[:, :width] + words[pl.ds(first, tile), :].astype(F32))
                / (total[:, width:] + 1.0)
            ).astype(BF16)
        out_ref[pl.ds(here, tile), :] = total
        return 0

    for j, out_ref in enumerate(out_refs):
        lax.fori_loop(0, part // tile, functools.partial(one, out_ref, j * part), 0)


def update(plan, values, total, codebook):
    more, last = total is not None, codebook is not None
    rows = len(values) * plan.groups * plan.side
    shape = (
        [jax.ShapeDtypeStruct((plan.owned // 2, plan.width), BF16)] * 2
        if last
        else [jax.ShapeDtypeStruct((plan.owned, 2 * plan.width), F32)]
    )
    scratch = [pltpu.VMEM((1, rows), jnp.int32)]
    if last:
        scratch += [pltpu.VMEM((plan.owned, plan.width), BF16), pltpu.SemaphoreType.DMA]
    return pl.pallas_call(
        functools.partial(update_kernel, plan, len(values), more, last),
        out_shape=shape,
        in_specs=[VMEM] * (len(values) + more) + [HBM] * last,
        out_specs=[VMEM] * len(shape),
        scratch_shapes=scratch,
        compiler_params=limit(20),
        cost_estimate=pl.CostEstimate(
            flops=4 * plan.owned * rows * plan.width,
            bytes_accessed=2 * rows * plan.width,
            transcendentals=0,
        ),
        name="update",
    )(*values, *([total] if more else []), *([codebook] if last else []))


def stage_kernel(plan, step, hold, held, n_block, n_carried, labels_ref, *refs):
    n_piece = 0 if hold else plan.n_sub
    pieces, refs = refs[:n_piece], refs[n_piece:]
    values_ref, near_ref, *refs = refs
    before, refs = (refs[0], refs[1:]) if held else (None, refs)
    blocks, refs = refs[:n_block], refs[n_block + n_carried :]
    centroid_ref, distance_ref, out_ref = refs[:3]
    table, picked, product, distance, sems, label_sems, *labels = refs[3:]
    values = (values_ref, near_ref)
    own, group, half = plan.here()
    sub = lax.axis_index("sub")
    high = lax.div(sub, plan.n_sub // 2)
    target = plan.target(step, group, half)
    width, side, rows, chunk = plan.width, plan.side, plan.rows, plan.chunk
    loads = [
        pltpu.make_async_copy(
            labels_ref.at[:, j * plan.groups + target, :], label, label_sems.at[j]
        )
        for j, label in enumerate(labels)
    ]
    for load in loads:
        load.start()
    size = blocks[0].shape[0]
    copies = []
    for j, block in enumerate(blocks):
        first = (half ^ (j // 2)) * (2 * size) + (j % 2) * size if n_block == 4 else 0
        first = pl.multiple_of(first, size)
        copies.append(
            pltpu.make_async_copy(
                block, centroid_ref.at[target, pl.ds(first, size), :], sems.at[j]
            )
        )
        copies[-1].start()
        table[pl.ds(first, size), :] = block[...].astype(F32)
    if not hold:
        product[...] = jnp.zeros_like(product)
    for load in loads:
        load.wait()
    batch = max(LANE // max(chunk // 512, 1), 8)

    def gather(p, slot):
        def some(b, _):
            for v in range(batch):
                lane = b * batch + v
                for j, label in enumerate(labels):
                    code = label[p, lane]
                    picked[slot, pl.ds(j * LANE + lane, 1), :] = table[pl.ds(code, 1), :]
            return 0

        if batch == LANE:
            some(0, 0)
        else:
            lax.fori_loop(0, LANE // batch, some, 0)

    def multiply(p, slot):
        if hold:
            out_ref[p] = picked[slot].astype(BF16)
            return
        left = jnp.concatenate([piece[p, : plan.band, :] for piece in pieces], axis=1)
        right = []
        for o in range(plan.n_sub):
            part = pl.ds(pl.multiple_of((sub ^ o) * rows, rows), rows)
            rebuilt = picked[slot, part, :].astype(BF16)
            if held:
                rebuilt = jnp.concatenate([rebuilt, before[p, part, :]], axis=1)
            right.append(rebuilt)
        product[...] += jnp.dot(left, jnp.concatenate(right, axis=0), preferred_element_type=F32)

    def measure(p, slot):
        @pl.when(p == own)
        def _():
            for part in range(2):
                first = pl.multiple_of((high ^ part) * side, side)
                gap = values[part][target].astype(F32) - picked[slot, pl.ds(first, side), :]
                distance[:, pl.ds(first, side)] = jnp.sum(
                    jnp.transpose(gap * gap), axis=0, keepdims=True
                )

    def both(i, _):
        gather(2 * i + 1, 1)
        multiply(2 * i, 0)
        measure(2 * i, 0)
        measure(2 * i + 1, 1)
        gather(2 * i + 2, 0)
        multiply(2 * i + 1, 1)
        return 0

    last = plan.n_dp - 1
    gather(0, 0)
    lax.fori_loop(0, last // 2, both, 0)
    gather(last, 1)
    multiply(last - 1, 0)
    measure(last - 1, 0)
    measure(last, 1)
    multiply(last, 1)
    if not hold:
        spots = [target, plan.target(step - 1, group, half)][: 1 + held]
        for j, spot in enumerate(spots):
            copies.append(
                pltpu.make_async_copy(
                    product.at[:, j * width : (j + 1) * width],
                    out_ref.at[:, pl.ds(pl.multiple_of(spot * width, width), width)],
                    sems.at[4 + j],
                )
            )
            copies[-1].start()
    copies.append(pltpu.make_async_copy(distance, distance_ref.at[pl.ds(target, 1), :], sems.at[6]))
    copies[-1].start()
    for copy in copies:
        copy.wait()


def stage(plan, step, hold, labels, pieces, values, before, blocks, carried):
    held = before is not None
    depth, total = plan.band, plan.n_dp * plan.chunk
    inputs = [*([] if hold else pieces), *values, *([before] if held else []), *blocks]
    fixed = 1 + len(inputs)
    if hold:
        last, last_spec = jax.ShapeDtypeStruct((plan.n_dp, plan.chunk, plan.width), BF16), VMEM
    else:
        last, last_spec = jax.ShapeDtypeStruct((depth, plan.groups * plan.width), F32), ANY
    return pl.pallas_call(
        functools.partial(stage_kernel, plan, step, hold, held, len(blocks), len(carried)),
        out_shape=(
            jax.ShapeDtypeStruct((plan.groups, plan.count, plan.width), BF16),
            jax.ShapeDtypeStruct((plan.groups, plan.chunk), F32),
            last,
        ),
        in_specs=[ANY] + [VMEM] * (fixed - 1) + [ANY] * len(carried),
        out_specs=(ANY, ANY, last_spec),
        scratch_shapes=[
            pltpu.VMEM((plan.count, plan.width), F32),
            pltpu.VMEM((2, plan.chunk, plan.width), F32),
            pltpu.VMEM((depth, (1 + held) * plan.width), F32),
            pltpu.VMEM((1, plan.chunk), F32),
            pltpu.SemaphoreType.DMA((7,)),
            pltpu.SemaphoreType.DMA((plan.chunk // LANE,)),
        ]
        + [pltpu.SMEM((plan.n_dp, LANE), jnp.int32)] * (plan.chunk // LANE),
        input_output_aliases={fixed + j: j for j in range(len(carried))},
        compiler_params=limit(10),
        cost_estimate=pl.CostEstimate(
            flops=2 * depth * plan.width * total * 32,
            bytes_accessed=4 * total * plan.width,
            transcendentals=0,
        ),
        name="stage",
    )(labels, *inputs, *carried)


def spread(own, size, axis):
    have = {0: own}
    bit = size // 2
    while bit:
        pairs = [(i, i ^ bit) for i in range(size)]
        for offset in sorted(have):
            have[offset ^ bit] = lax.ppermute(have[offset], axis, pairs)
        bit //= 2
    return [have[o] for o in range(size)]


def per_device(n_dp, n_sub, vectors, rotation, codebook, codes):
    plan = Plan(n_dp, n_sub, codebook, vectors)
    groups, halves, ring = plan.groups, plan.halves, plan.ring
    turning = flip(plan, vectors, codes.T)
    pieces = spread(vectors, n_sub, "sub")
    near, far = list(range(n_sub // 2)), list(range(n_sub // 2, n_sub))
    values = [rotate(plan, 0, near, pieces[: n_sub // 2], rotation, codes.T, 58)]
    values += [rotate(plan, 1, far, pieces[n_sub // 2 :], rotation, codes.T, 10)]

    def partner(p, t):
        g, h = p // halves, p % halves
        return ring[(g ^ t) * halves + (h ^ plan.mirror(g) ^ plan.mirror(g ^ t))]

    joined = []
    for part in range(2):
        got = [values[part][1]]
        for t in range(1, groups):
            pairs = [(ring[p], partner(p, t)) for p in range(n_dp)]
            got.append(lax.ppermute(values[part][t + 1], "dp", pairs))
        held = {0: pack(got)}
        bit = 1
        while bit < halves:
            pairs = [
                (ring[p], ring[(p // halves) * halves + ((p % halves) ^ bit)]) for p in range(n_dp)
            ]
            for e in sorted(held):
                held[e ^ bit] = lax.ppermute(held[e], "dp", pairs)
            bit *= 2
        joined.append(held)

    turned = lax.all_to_all(turning, "dp", 0, 0, tiled=True)
    sides = spread(turned, n_sub, "sub")
    digits = turned[:, plan.band :, :].astype(jnp.int32).reshape(n_dp, 2, -1, LANE)
    labels = digits[:, 0] * LANE + digits[:, 1]

    arrays = [joined[part][e] for part in range(2) for e in sorted(joined[part])]
    (total,) = update(plan, arrays[:-1], None, None)
    block = update(plan, arrays[-1:], total, codebook)

    own = [v[0] for v in values]
    carried, before = (), None
    if plan.paired:
        inner = [(ring[p], ring[p ^ 1]) for p in range(n_dp)]
        outer = [(ring[p], ring[(p - 1 if p % 2 == 0 else p + 1) % n_dp]) for p in range(n_dp)]
        a, b = block, block
        for s in range(1, groups + 1):
            if s < groups:
                a_next = [lax.ppermute(x, "dp", inner) for x in b]
                b_next = [lax.ppermute(x, "dp", outer) for x in a]
            else:
                a_next = [lax.ppermute(b[0], "dp", inner), lax.ppermute(a[1], "dp", outer)]
                b_next = a_next
            found = [*a, *a_next] if s % 2 else [*b_next, *b]
            a, b = a_next, b_next
            hold = s == 1 and groups > 1
            carried = stage(plan, s, hold, labels, sides, own, before, found, carried)
            before = None
            if hold:
                *carried, before = carried
    else:
        table = lax.all_gather(jnp.concatenate(block, axis=0), "dp", axis=0, tiled=True)
        table = table.reshape(groups, plan.count, plan.width)
        for g in range(groups):
            carried = stage(plan, g + 1, False, labels, sides, own, None, [table[g]], carried)
    centroid, distance, cross = carried
    return centroid, distance.T, cross


def solution(mesh):
    placed = (P(("dp", "sub"), None), P(None, "sub"), P("sub", None, None), P("dp", "sub"))
    return jax.shard_map(
        functools.partial(per_device, mesh.shape["dp"], mesh.shape["sub"]),
        mesh=mesh,
        in_specs=placed,
        out_specs=(P("sub", None, None), P("dp", "sub"), P("dp", "sub")),
        check_vma=False,
    )
```
